768 devices in a mesh: dp: 192 (over z, y_hi, x, core), slab: 4 (over y_lo).
Axes of the slice: x: 4, y: 8 (y_hi: 2, y_lo: 4; y = y_hi * 4 + y_lo), z: 12, core: 2. Of those that a mesh axis runs over, the one named last changes fastest.
Arguments:
- gradient: bfloat16 [192, 3584, 1024], P('dp', 'slab'), may hold values from -500 to 500
Outputs:
- update: bfloat16 [192, 3584, 1024], P('dp', 'slab')
- grad_rms: float32 [], replicated
The draws below stay inside these ranges and needn't reach their ends.
All inputs are finite; a program needn't handle non-finite values.
Results may differ from the reference program's by a relative error of at most 0.0034.
Values may be sent and summed in bfloat16 or wider, within the bound.
No kernel may reach another device: no remote copies, remote signals or barrier semaphores. Data moves between devices by JAX's collectives and lax.ppermute only.
A program may use at most 32 MiB of HBM per device.

```python
import math
import jax
import jax.numpy as jnp
from jax import lax

R = 3584
C = 1024
EXPERTS = 192
N_SLAB = 4


def draw_gradient(key, part):
    noise_key, row_key, col_key = jax.random.split(key, 3)
    rand_noise = jax.random.truncated_normal(noise_key, -6.0, 6.0, (EXPERTS, R, C), jnp.float32)
    row_scale = jnp.exp(jax.random.uniform(row_key, (EXPERTS, R, 1), jnp.float32, math.log(0.3), math.log(3.0)))
    col_scale = jnp.exp(jax.random.uniform(col_key, (EXPERTS, 1, C), jnp.float32, math.log(0.3), math.log(3.0)))
    expert_pos = jnp.arange(EXPERTS, dtype=jnp.float32) / max(EXPERTS - 1, 1)
    row_pos = jnp.arange(R, dtype=jnp.float32) / max(R - 1, 1)
    expert_rise = 1.0 + 2.0 * expert_pos
    row_rise = 1.0 + 2.0 * row_pos
    growth = expert_rise[:, None, None] * row_rise[None, :, None]
    return (0.1 * rand_noise * row_scale * col_scale * growth).astype(jnp.bfloat16)


def setup_inputs(seed: int = 0) -> dict:
    arg_keys = jax.random.split(jax.random.key(seed), 2)
    gradient = draw_gradient(jax.random.fold_in(arg_keys[1], 71), 0)
    return dict(gradient=gradient)


def block_gram(slab_block):
    product = lax.dot_general(slab_block, slab_block, (((0,), (0,)), ((), ())), preferred_element_type=jnp.float32)
    return product.astype(jnp.bfloat16)

def expert_step(matrix):
    blocks = matrix.reshape(N_SLAB, R // N_SLAB, C)
    partials = lax.map(block_gram, blocks)
    gram = lax.optimization_barrier(jnp.sum(partials.astype(jnp.float32), axis=0)).astype(jnp.bfloat16)
    gram_wide = gram.astype(jnp.float32)
    norm_gram = jnp.sqrt(jnp.sum(gram_wide * gram_wide))
    factor = 1.0 / (norm_gram + 1e-07)
    squared = jnp.dot(gram, gram, preferred_element_type=jnp.float32)
    poly = (-4.775 * factor * gram_wide + 2.0315 * factor * factor * squared).astype(jnp.bfloat16)
    applied = jnp.dot(matrix, poly, preferred_element_type=jnp.float32)
    update = (math.sqrt(R) * jnp.sqrt(factor) * (3.4445 * matrix.astype(jnp.float32) + applied)).astype(jnp.bfloat16)
    matrix_wide = matrix.astype(jnp.float32)
    squares = jnp.sum(matrix_wide * matrix_wide)
    return (update, squares)

def reference(gradient):
    updates, squares = lax.map(expert_step, gradient)
    grad_rms = jnp.sqrt(jnp.sum(squares) / (EXPERTS * R * C))
    return (updates, grad_rms)
```

```python
import functools
import math

import jax
import jax.numpy as jnp
from jax import lax
from jax.experimental import pallas as pl
from jax.experimental.pallas import tpu as pltpu
from jax.sharding import PartitionSpec as P

R = 3584
C = 1024
B = 256
H = 128
ROWS = 2 * B + 16

FULL = ((1, 0), (2, 1), (3, 2), (3, 0))
HALF = ((2, 0, 0), (2, 0, 1), (3, 1, 0), (3, 1, 1))


def pick(p, values):
    out = jnp.int32(values[0])
    for k in range(1, len(values)):
        out = jnp.where(p == k, jnp.int32(values[k]), out)
    return out


def lower(shape=(H, H)):
    rows = lax.broadcasted_iota(jnp.int32, shape, 0)
    cols = lax.broadcasted_iota(jnp.int32, shape, 1)
    return rows, cols


def columns(x_ref, start, width):
    return x_ref[0, :, pl.ds(pl.multiple_of(start, H), width)]


def outer(a, b):
    return lax.dot_general(a, b, (((0,), (0,)), ((), ())), preferred_element_type=jnp.float32)


def encode(total):
    hi = total.astype(jnp.bfloat16)
    rest = total - hi.astype(jnp.float32)
    mid = rest.astype(jnp.bfloat16)
    low = (rest - mid.astype(jnp.float32)).astype(jnp.bfloat16)
    return hi, mid, low


def decode(extras):
    wide = extras.astype(jnp.float32)
    return wide[1:2, :] + wide[2:3, :] + wide[3:4, :]


def extras_of(diagonal, total):
    hi, mid, low = encode(total)
    row = lax.broadcasted_iota(jnp.int32, (16, B), 0)
    out = jnp.where(row == 0, diagonal, 0.0)
    for k, part in ((1, hi), (2, mid), (3, low)):
        out = jnp.where(row == k, part.astype(jnp.float32), out)
    return out.astype(jnp.bfloat16)


def quarter(x_ref, p, total, out_ref):
    own = columns(x_ref, p * B, B)
    diag = outer(own, own)
    fi, fj = (pick(p, [f[k] for f in FULL]) for k in (0, 1))
    out_ref[0:B, :] = outer(columns(x_ref, fi * B, B), columns(x_ref, fj * B, B)).astype(jnp.bfloat16)
    hi, hj, part = (pick(p, [h[k] for h in HALF]) for k in (0, 1, 2))
    out_ref[B : B + H, :] = outer(
        columns(x_ref, hi * B + part * H, H), columns(x_ref, hj * B, B)
    ).astype(jnp.bfloat16)
    rows, cols = lower()
    first, last = diag[:H, :H], diag[H:, H:]
    out_ref[B + H : 2 * B, :H] = diag[H:, :H].astype(jnp.bfloat16)
    out_ref[B + H : 2 * B, H:] = jnp.where(rows > cols, first, last).astype(jnp.bfloat16)
    line = jnp.sum(jnp.where(rows == cols, first, 0.0), axis=0, keepdims=True)
    out_ref[2 * B :, :] = extras_of(jnp.concatenate([line, line], axis=1), total)


def first_kernel(own_ref, x_ref, out_ref, sum_ref):
    wide = x_ref[0].astype(jnp.float32)
    squares = jnp.sum(wide * wide, axis=0, keepdims=True)
    total = jnp.sum(squares, axis=1, keepdims=True)
    total = jnp.broadcast_to(total, (1, B))
    sum_ref[...] = jnp.broadcast_to(total[:, :H], (8, H))
    quarter(x_ref, 2 * (1 - own_ref[0]), total, out_ref)


def second_kernel(own_ref, x_ref, sum_ref, send_ref, keep0_ref, keep1_ref):
    own = own_ref[0]
    total = jnp.broadcast_to(sum_ref[0:1, 0:1], (1, B))
    quarter(x_ref, 2 * (1 - own) + 1, total, send_ref)
    quarter(x_ref, 2 * own, total, keep0_ref)
    quarter(x_ref, 2 * own + 1, total, keep1_ref)


def add_kernel(a_ref, b_ref, out_ref, sum_ref):
    body = slice(0, 2 * B)
    out_ref[body, :] = (a_ref[body, :].astype(jnp.float32) + b_ref[body, :].astype(jnp.float32)).astype(jnp.bfloat16)
    a, b = a_ref[2 * B :, :], b_ref[2 * B :, :]
    total = decode(a) + decode(b)
    out_ref[2 * B :, :] = extras_of(a[0:1, :].astype(jnp.float32) + b[0:1, :].astype(jnp.float32), total)
    sum_ref[...] = jnp.broadcast_to(total[:, :H], (8, H))


def final_kernel(own_ref, k0_ref, k1_ref, r0_ref, r1_ref, x_ref, out_ref, gram, poly, scale):
    @pl.when(pl.program_id(0) == 0)
    def _():
        mine = own_ref[0] == 0
        kept, received = (k0_ref, k1_ref), (r0_ref, r1_ref)
        rows, cols = lower()
        squares = jnp.zeros((H, B), jnp.float32)
        for p in range(4):
            keep, recv = kept[p % 2], received[p % 2]
            low = p < 2

            def get(part):
                k, r = keep[part, :], recv[part, :]
                return jnp.where(mine, k, r) if low else jnp.where(mine, r, k)

            def put(i, j, block):
                gram[i : i + block.shape[0], j : j + block.shape[1]] = block
                gram[j : j + block.shape[1], i : i + block.shape[0]] = block.T

            block = get(slice(0, B))
            fi, fj = FULL[p]
            put(fi * B, fj * B, block)
            wide = block.astype(jnp.float32)
            squares += 2.0 * (wide[:H] * wide[:H] + wide[H:] * wide[H:])
            block = get(slice(B, B + H))
            hi, hj, part = HALF[p]
            put(hi * B + part * H, hj * B, block)
            wide = block.astype(jnp.float32)
            squares += 2.0 * wide * wide
            block = get(slice(B + H, 2 * B))
            put(p * B + H, p * B, block[:, :H])
            fold = block[:, H:].astype(jnp.float32)
            flip = fold.T
            line = get(slice(2 * B, 2 * B + 16))[0:1, :H].astype(jnp.float32)
            upper = jnp.where(rows < cols, flip, jnp.where(rows == cols, jnp.broadcast_to(line, (H, H)), fold))
            second = jnp.where(rows > cols, flip, fold)
            gram[p * B : p * B + H, p * B : p * B + H] = upper.astype(jnp.bfloat16)
            gram[p * B + H : (p + 1) * B, p * B + H : (p + 1) * B] = second.astype(jnp.bfloat16)
            wide = block[:, :H].astype(jnp.float32)
            squares += jnp.concatenate([2.0 * wide * wide, upper * upper + second * second], axis=1)
        norm = jnp.sqrt(jnp.sum(jnp.sum(squares, axis=0, keepdims=True), axis=1, keepdims=True))
        factor = 1.0 / (norm + 1e-07)
        scale[...] = jnp.broadcast_to(math.sqrt(R) * jnp.sqrt(factor), (8, H))
        for i in range(4):
            for j in range(i + 1):
                product = jnp.dot(
                    gram[i * B : (i + 1) * B, :], gram[:, j * B : (j + 1) * B], preferred_element_type=jnp.float32
                )
                block = gram[i * B : (i + 1) * B, j * B : (j + 1) * B].astype(jnp.float32)
                block = (-4.775 * factor * block + 2.0315 * factor * factor * product).astype(jnp.bfloat16)
                poly[i * B : (i + 1) * B, j * B : (j + 1) * B] = block
                if i != j:
                    poly[j * B : (j + 1) * B, i * B : (i + 1) * B] = block.T

    x = x_ref[0]
    applied = jnp.dot(x, poly[...], preferred_element_type=jnp.float32)
    out_ref[0] = (scale[0:1, 0:1] * (3.4445 * x.astype(jnp.float32) + applied)).astype(jnp.bfloat16)


PIECE = jax.ShapeDtypeStruct((ROWS, B), jnp.bfloat16)
TILE = jax.ShapeDtypeStruct((8, H), jnp.float32)
SMEM = pl.BlockSpec(memory_space=pltpu.SMEM)
VMEM = pl.BlockSpec(memory_space=pltpu.VMEM)


def call(kernel, n_in, outs, flops, nbytes):
    return pl.pallas_call(
        kernel,
        out_shape=outs,
        in_specs=[SMEM] + [VMEM] * n_in,
        out_specs=[VMEM] * len(outs),
        cost_estimate=pl.CostEstimate(flops=flops, bytes_accessed=nbytes, transcendentals=0),
        compiler_params=pltpu.CompilerParams(vmem_limit_bytes=16 << 20),
    )


def add_pieces(a, b):
    return pl.pallas_call(
        add_kernel,
        out_shape=[PIECE, TILE],
        in_specs=[VMEM] * 2,
        out_specs=[VMEM] * 2,
        cost_estimate=pl.CostEstimate(flops=ROWS * B, bytes_accessed=6 * ROWS * B, transcendentals=0),
        compiler_params=pltpu.CompilerParams(vmem_limit_bytes=4 << 20),
    )(a, b)


def finish(own, k0, k1, r0, r1, x, rows):
    step = 128
    return pl.pallas_call(
        final_kernel,
        grid=(rows // step,),
        out_shape=jax.ShapeDtypeStruct((1, rows, C), jnp.bfloat16),
        in_specs=[SMEM] + [VMEM] * 4 + [pl.BlockSpec((1, step, C), lambda i: (0, i, 0))],
        out_specs=pl.BlockSpec((1, step, C), lambda i: (0, i, 0)),
        scratch_shapes=[
            pltpu.VMEM((C, C), jnp.bfloat16),
            pltpu.VMEM((C, C), jnp.bfloat16),
            pltpu.VMEM((8, H), jnp.float32),
        ],
        cost_estimate=pl.CostEstimate(flops=4 * rows * C * C, bytes_accessed=4 * rows * C, transcendentals=0),
        compiler_params=pltpu.CompilerParams(vmem_limit_bytes=24 << 20),
    )(own, k0, k1, r0, r1, x)


PAIR = [(0, 1), (1, 0), (2, 3), (3, 2)]
CROSS = [(1, 2), (2, 1), (0, 3), (3, 0)]
Z, YH, X, CORES = 12, 2, 4, 2


def moved(dz=0, flip=False, dx=0, other=False):
    pairs = []
    for z in range(Z):
        for yh in range(YH):
            for x in range(X):
                for c in range(CORES):
                    src = ((z * YH + yh) * X + x) * CORES + c
                    to = (((z + dz) % Z * YH + yh ^ flip) * X + (x + dx) % X) * CORES + (c ^ other)
                    pairs.append((src, to))
    return pairs


def spread(total):
    for shifts in (
        [moved(other=True)],
        [moved(dx=1)],
        [moved(dx=2)],
        [moved(dz=4), moved(dz=8)],
        [moved(dz=2)],
        [moved(dz=1)],
        [moved(flip=True)],
    ):
        total = functools.reduce(jnp.add, [lax.ppermute(total, "dp", s) for s in shifts], total)
    return total


def shards(gradient):
    rows = gradient.shape[1]
    place = lax.axis_index("slab")
    own = jnp.where((place == 1) | (place == 2), 1, 0).astype(jnp.int32).reshape(1)
    send0, tile = call(first_kernel, 1, [PIECE, TILE], rows * B * B * 5, 2 * rows * C)(own, gradient)
    got0 = lax.ppermute(send0, "slab", PAIR)
    send1, keep0, keep1 = call(second_kernel, 2, [PIECE] * 3, rows * B * B * 15, 2 * rows * C)(own, gradient, tile)
    got1 = lax.ppermute(send1, "slab", PAIR)
    half0, _ = add_pieces(keep0, got0)
    cross0 = lax.ppermute(half0, "slab", CROSS)
    half1, _ = add_pieces(keep1, got1)
    cross1 = lax.ppermute(half1, "slab", CROSS)
    whole0, total = add_pieces(half0, cross0)
    other0 = lax.ppermute(whole0, "slab", PAIR)
    whole1, _ = add_pieces(half1, cross1)
    other1 = lax.ppermute(whole1, "slab", PAIR)
    update = finish(own, whole0, whole1, other0, other1, gradient, rows)
    total = spread(total)
    entries = gradient.size * lax.axis_size("dp") * lax.axis_size("slab")
    return update, jnp.sqrt(total[0, 0] / entries)


def solution(mesh):
    return jax.shard_map(
        shards, mesh=mesh, in_specs=(P("dp", "slab", None),), out_specs=(P("dp", "slab", None), P()), check_vma=False
    )
```

```python
import math

import jax
import jax.numpy as jnp
from jax import lax
from jax.experimental import pallas as pl
from jax.experimental.pallas import tpu as pltpu
from jax.sharding import Mesh
from jax.sharding import PartitionSpec as P

R = 3584
C = 1024
B = 256
H = 128
ROWS = 2 * B + 16

FULL = ((1, 0), (2, 1), (3, 2), (3, 0))
HALF = ((2, 0, 0), (2, 0, 1), (3, 1, 0), (3, 1, 1))


def pick(p, values):
    out = jnp.int32(values[0])
    for k in range(1, len(values)):
        out = jnp.where(p == k, jnp.int32(values[k]), out)
    return out


def lower(shape=(H, H)):
    rows = lax.broadcasted_iota(jnp.int32, shape, 0)
    cols = lax.broadcasted_iota(jnp.int32, shape, 1)
    return rows, cols


def columns(x_ref, start, width):
    return x_ref[0, :, pl.ds(pl.multiple_of(start, H), width)]


def outer(a, b):
    return lax.dot_general(a, b, (((0,), (0,)), ((), ())), preferred_element_type=jnp.float32)


def quarter(x_ref, p, out_ref, slot):
    own = columns(x_ref, p * B, B)
    diag = outer(own, own)
    fi, fj = (pick(p, [f[k] for f in FULL]) for k in (0, 1))
    out_ref[slot, 0:B, :] = outer(columns(x_ref, fi * B, B), columns(x_ref, fj * B, B)).astype(jnp.bfloat16)
    hi, hj, part = (pick(p, [h[k] for h in HALF]) for k in (0, 1, 2))
    out_ref[slot, B : B + H, :] = outer(
        columns(x_ref, hi * B + part * H, H), columns(x_ref, hj * B, B)
    ).astype(jnp.bfloat16)
    rows, cols = lower()
    first, last = diag[:H, :H], diag[H:, H:]
    out_ref[slot, B + H : 2 * B, :H] = diag[H:, :H].astype(jnp.bfloat16)
    out_ref[slot, B + H : 2 * B, H:] = jnp.where(rows > cols, first, last).astype(jnp.bfloat16)
    line = jnp.sum(jnp.where(rows == cols, first, 0.0), axis=0, keepdims=True)
    line = jnp.broadcast_to(jnp.concatenate([line, line], axis=1), (16, B))
    out_ref[slot, 2 * B :, :] = line.astype(jnp.bfloat16)


def first_kernel(own_ref, x_ref, out_ref, sum_ref):
    wide = x_ref[0].astype(jnp.float32)
    squares = jnp.sum(wide * wide, axis=0, keepdims=True)
    total = jnp.sum(squares, axis=1, keepdims=True)
    sum_ref[...] = jnp.broadcast_to(total, (8, H))
    for slot in range(2):
        quarter(x_ref, 2 * (1 - own_ref[0]) + slot, out_ref, slot)


def second_kernel(own_ref, x_ref, keep_ref):
    for slot in range(2):
        quarter(x_ref, 2 * own_ref[0] + slot, keep_ref, slot)


def add_kernel(a_ref, b_ref, out_ref):
    out_ref[...] = (a_ref[...].astype(jnp.float32) + b_ref[...].astype(jnp.float32)).astype(jnp.bfloat16)


def final_kernel(own_ref, keep_ref, recv_ref, x_ref, out_ref, gram, poly, scale):
    @pl.when(pl.program_id(0) == 0)
    def _():
        mine = own_ref[0] == 0
        rows, cols = lower()
        squares = jnp.zeros((H, B), jnp.float32)
        for p in range(4):
            slot, low = p % 2, p < 2

            def get(part):
                k, r = keep_ref[slot, part, :], recv_ref[slot, part, :]
                return jnp.where(mine, k, r) if low else jnp.where(mine, r, k)

            def put(i, j, block):
                gram[i : i + block.shape[0], j : j + block.shape[1]] = block
                gram[j : j + block.shape[1], i : i + block.shape[0]] = block.T

            block = get(slice(0, B))
            fi, fj = FULL[p]
            put(fi * B, fj * B, block)
            wide = block.astype(jnp.float32)
            squares += 2.0 * (wide[:H] * wide[:H] + wide[H:] * wide[H:])
            block = get(slice(B, B + H))
            hi, hj, part = HALF[p]
            put(hi * B + part * H, hj * B, block)
            wide = block.astype(jnp.float32)
            squares += 2.0 * wide * wide
            block = get(slice(B + H, 2 * B))
            put(p * B + H, p * B, block[:, :H])
            fold = block[:, H:].astype(jnp.float32)
            flip = fold.T
            line = get(slice(2 * B, 2 * B + 16))[0:1, :H].astype(jnp.float32)
            upper = jnp.where(rows < cols, flip, jnp.where(rows == cols, jnp.broadcast_to(line, (H, H)), fold))
            second = jnp.where(rows > cols, flip, fold)
            gram[p * B : p * B + H, p * B : p * B + H] = upper.astype(jnp.bfloat16)
            gram[p * B + H : (p + 1) * B, p * B + H : (p + 1) * B] = second.astype(jnp.bfloat16)
            wide = block[:, :H].astype(jnp.float32)
            squares += jnp.concatenate([2.0 * wide * wide, upper * upper + second * second], axis=1)
        norm = jnp.sqrt(jnp.sum(jnp.sum(squares, axis=0, keepdims=True), axis=1, keepdims=True))
        factor = 1.0 / (norm + 1e-07)
        scale[...] = jnp.broadcast_to(math.sqrt(R) * jnp.sqrt(factor), (8, H))
        for i in range(4):
            for j in range(i + 1):
                product = jnp.dot(
                    gram[i * B : (i + 1) * B, :], gram[:, j * B : (j + 1) * B], preferred_element_type=jnp.float32
                )
                block = gram[i * B : (i + 1) * B, j * B : (j + 1) * B].astype(jnp.float32)
                block = (-4.775 * factor * block + 2.0315 * factor * factor * product).astype(jnp.bfloat16)
                poly[i * B : (i + 1) * B, j * B : (j + 1) * B] = block
                if i != j:
                    poly[j * B : (j + 1) * B, i * B : (i + 1) * B] = block.T

    x = x_ref[0]
    applied = jnp.dot(x, poly[...], preferred_element_type=jnp.float32)
    out_ref[0] = (scale[0:1, 0:1] * (3.4445 * x.astype(jnp.float32) + applied)).astype(jnp.bfloat16)


HALVES = jax.ShapeDtypeStruct((2, ROWS, B), jnp.bfloat16)
TILE = jax.ShapeDtypeStruct((8, H), jnp.float32)
SMEM = pl.BlockSpec(memory_space=pltpu.SMEM)
VMEM = pl.BlockSpec(memory_space=pltpu.VMEM)


def call(kernel, in_specs, outs, flops, nbytes, limit):
    return pl.pallas_call(
        kernel,
        out_shape=outs,
        in_specs=in_specs,
        out_specs=[VMEM] * len(outs),
        cost_estimate=pl.CostEstimate(flops=flops, bytes_accessed=nbytes, transcendentals=0),
        compiler_params=pltpu.CompilerParams(vmem_limit_bytes=limit << 20),
    )


def add_halves(a, b):
    return call(add_kernel, [VMEM] * 2, [HALVES], 2 * ROWS * B, 12 * ROWS * B, 8)(a, b)[0]


def finish(own, keep, recv, x, rows):
    step = 128
    return pl.pallas_call(
        final_kernel,
        grid=(rows // step,),
        out_shape=jax.ShapeDtypeStruct((1, rows, C), jnp.bfloat16),
        in_specs=[SMEM] + [VMEM] * 2 + [pl.BlockSpec((1, step, C), lambda i: (0, i, 0))],
        out_specs=pl.BlockSpec((1, step, C), lambda i: (0, i, 0)),
        scratch_shapes=[
            pltpu.VMEM((C, C), jnp.bfloat16),
            pltpu.VMEM((C, C), jnp.bfloat16),
            pltpu.VMEM((8, H), jnp.float32),
        ],
        cost_estimate=pl.CostEstimate(flops=4 * rows * C * C, bytes_accessed=4 * rows * C, transcendentals=0),
        compiler_params=pltpu.CompilerParams(vmem_limit_bytes=24 << 20),
    )(own, keep, recv, x)


PAIR = [(0, 1), (1, 0), (2, 3), (3, 2)]
CROSS = [(1, 2), (2, 1), (0, 3), (3, 0)]
DP = ("z", "y_hi", "x", "core")
Z, Y_HI, X, CORES = 12, 2, 4, 2


def over(line, axes):
    count = lax.axis_size(axes)
    parts = lax.all_to_all(jnp.broadcast_to(line, (count, H)), axes, 0, 0, tiled=True)
    return jnp.sum(parts, axis=0, keepdims=True)


def shards(gradient):
    rows = gradient.shape[1]
    place = lax.axis_index("slab")
    own = jnp.where((place == 1) | (place == 2), 1, 0).astype(jnp.int32).reshape(1)
    work = rows * B * B * 10
    send, tile = call(first_kernel, [SMEM, VMEM], [HALVES, TILE], work, 2 * rows * C, 16)(own, gradient)
    got = lax.ppermute(send, "slab", PAIR)
    (keep,) = call(second_kernel, [SMEM, VMEM], [HALVES], work, 2 * rows * C, 16)(own, gradient)
    total = over(tile[0:1], ("x", "core"))
    got, total = lax.optimization_barrier((got, total))
    half = add_halves(keep, got)
    crossed = lax.ppermute(half, "slab", CROSS)
    half, total = lax.optimization_barrier((half, total))
    total = over(total, ("z",))
    crossed, total = lax.optimization_barrier((crossed, total))
    whole = add_halves(half, crossed)
    other = lax.ppermute(whole, "slab", PAIR)
    whole, total = lax.optimization_barrier((whole, total))
    total = over(total, ("y_hi", "slab"))
    other, total = lax.optimization_barrier((other, total))
    update = finish(own, whole, other, gradient, rows)
    entries = gradient.size * lax.axis_size(DP) * lax.axis_size("slab")
    return update, jnp.sqrt(total[0, 0] / entries)


def solution(mesh):
    named = Mesh(mesh.devices.reshape(Z, Y_HI, X, CORES, mesh.shape["slab"]), DP + ("slab",))
    placed = P(DP, "slab", None)
    return jax.shard_map(shards, mesh=named, in_specs=(placed,), out_specs=(placed, P()), check_vma=False)
```

```python
import math

import jax
import jax.numpy as jnp
from jax import lax
from jax.experimental import pallas as pl
from jax.experimental.pallas import tpu as pltpu
from jax.sharding import Mesh
from jax.sharding import PartitionSpec as P

R = 3584
C = 1024
B = 256
H = 128
REST = B + 16
LARGE = 2 * B + REST

FULL = ((1, 0), (2, 1), (3, 2), (3, 0))
HALF = ((2, 0, 0), (2, 0, 1), (3, 1, 0), (3, 1, 1))


def pick(p, values):
    out = jnp.int32(values[0])
    for k in range(1, len(values)):
        out = jnp.where(p == k, jnp.int32(values[k]), out)
    return out


def lower(shape=(H, H)):
    rows = lax.broadcasted_iota(jnp.int32, shape, 0)
    cols = lax.broadcasted_iota(jnp.int32, shape, 1)
    return rows, cols


def columns(x_ref, start, width):
    return x_ref[0, :, pl.ds(pl.multiple_of(start, H), width)]


def outer(a, b):
    return lax.dot_general(a, b, (((0,), (0,)), ((), ())), preferred_element_type=jnp.float32)


def whole_block(x_ref, p, out_ref, at):
    i, j = (pick(p, [f[k] for f in FULL]) for k in (0, 1))
    out_ref[at : at + B, :] = outer(columns(x_ref, i * B, B), columns(x_ref, j * B, B)).astype(jnp.bfloat16)


def rest(x_ref, p, out_ref, at):
    i, j, part = (pick(p, [h[k] for h in HALF]) for k in (0, 1, 2))
    out_ref[at : at + H, :] = outer(
        columns(x_ref, i * B + part * H, H), columns(x_ref, j * B, B)
    ).astype(jnp.bfloat16)
    own = columns(x_ref, p * B, B)
    diag = outer(own, own)
    rows, cols = lower()
    first, last = diag[:H, :H], diag[H:, H:]
    out_ref[at + H : at + B, :H] = diag[H:, :H].astype(jnp.bfloat16)
    out_ref[at + H : at + B, H:] = jnp.where(rows > cols, first, last).astype(jnp.bfloat16)
    line = jnp.sum(jnp.where(rows == cols, first, 0.0), axis=0, keepdims=True)
    line = jnp.broadcast_to(jnp.concatenate([line, line], axis=1), (16, B))
    out_ref[at + B : at + REST, :] = line.astype(jnp.bfloat16)


def large_part(x_ref, half, out_ref):
    whole_block(x_ref, 2 * half, out_ref, 0)
    rest(x_ref, 2 * half, out_ref, B)
    whole_block(x_ref, 2 * half + 1, out_ref, B + REST)


def first_kernel(own_ref, x_ref, out_ref, sum_ref):
    wide = x_ref[0].astype(jnp.float32)
    squares = jnp.sum(wide * wide, axis=0, keepdims=True)
    total = jnp.sum(squares, axis=1, keepdims=True)
    sum_ref[...] = jnp.broadcast_to(total, (8, H))
    large_part(x_ref, 1 - own_ref[0], out_ref)


def second_kernel(own_ref, x_ref, out_ref):
    rest(x_ref, 2 * (1 - own_ref[0]) + 1, out_ref, 0)


def third_kernel(own_ref, x_ref, keep_a_ref, keep_b_ref):
    large_part(x_ref, own_ref[0], keep_a_ref)
    rest(x_ref, 2 * own_ref[0] + 1, keep_b_ref, 0)


def add_kernel(a_ref, b_ref, out_ref):
    out_ref[...] = (a_ref[...].astype(jnp.float32) + b_ref[...].astype(jnp.float32)).astype(jnp.bfloat16)


def final_kernel(own_ref, keep_a_ref, keep_b_ref, recv_a_ref, recv_b_ref, x_ref, out_ref, gram, poly, scale):
    @pl.when(pl.program_id(0) == 0)
    def _():
        mine = own_ref[0] == 0
        rows, cols = lower()
        squares = jnp.zeros((H, B), jnp.float32)
        for p in range(4):
            low = p < 2

            def get(small, start, size):
                keep_ref, recv_ref = (keep_b_ref, recv_b_ref) if small else (keep_a_ref, recv_a_ref)
                k, r = keep_ref[start : start + size, :], recv_ref[start : start + size, :]
                return jnp.where(mine, k, r) if low else jnp.where(mine, r, k)

            small = p % 2 == 1
            top, base = (B + REST, 0) if small else (0, B)

            def put(i, j, block):
                gram[i : i + block.shape[0], j : j + block.shape[1]] = block
                gram[j : j + block.shape[1], i : i + block.shape[0]] = block.T

            block = get(False, top, B)
            fi, fj = FULL[p]
            put(fi * B, fj * B, block)
            wide = block.astype(jnp.float32)
            squares += 2.0 * (wide[:H] * wide[:H] + wide[H:] * wide[H:])
            block = get(small, base, H)
            hi, hj, part = HALF[p]
            put(hi * B + part * H, hj * B, block)
            wide = block.astype(jnp.float32)
            squares += 2.0 * wide * wide
            block = get(small, base + H, H)
            put(p * B + H, p * B, block[:, :H])
            fold = block[:, H:].astype(jnp.float32)
            flip = fold.T
            line = get(small, base + B, 16)[0:1, :H].astype(jnp.float32)
            upper = jnp.where(rows < cols, flip, jnp.where(rows == cols, jnp.broadcast_to(line, (H, H)), fold))
            second = jnp.where(rows > cols, flip, fold)
            gram[p * B : p * B + H, p * B : p * B + H] = upper.astype(jnp.bfloat16)
            gram[p * B + H : (p + 1) * B, p * B + H : (p + 1) * B] = second.astype(jnp.bfloat16)
            wide = block[:, :H].astype(jnp.float32)
            squares += jnp.concatenate([2.0 * wide * wide, upper * upper + second * second], axis=1)
        norm = jnp.sqrt(jnp.sum(jnp.sum(squares, axis=0, keepdims=True), axis=1, keepdims=True))
        factor = 1.0 / (norm + 1e-07)
        scale[...] = jnp.broadcast_to(math.sqrt(R) * jnp.sqrt(factor), (8, H))
        for i in range(4):
            for j in range(i + 1):
                product = jnp.dot(
                    gram[i * B : (i + 1) * B, :], gram[:, j * B : (j + 1) * B], preferred_element_type=jnp.float32
                )
                block = gram[i * B : (i + 1) * B, j * B : (j + 1) * B].astype(jnp.float32)
                block = (-4.775 * factor * block + 2.0315 * factor * factor * product).astype(jnp.bfloat16)
                poly[i * B : (i + 1) * B, j * B : (j + 1) * B] = block
                if i != j:
                    poly[j * B : (j + 1) * B, i * B : (i + 1) * B] = block.T

    x = x_ref[0]
    applied = jnp.dot(x, poly[...], preferred_element_type=jnp.float32)
    out_ref[0] = (scale[0:1, 0:1] * (3.4445 * x.astype(jnp.float32) + applied)).astype(jnp.bfloat16)


PART_A = jax.ShapeDtypeStruct((LARGE, B), jnp.bfloat16)
PART_B = jax.ShapeDtypeStruct((REST, B), jnp.bfloat16)
TILE = jax.ShapeDtypeStruct((8, H), jnp.float32)
SMEM = pl.BlockSpec(memory_space=pltpu.SMEM)
VMEM = pl.BlockSpec(memory_space=pltpu.VMEM)


def call(kernel, in_specs, outs, flops, nbytes, limit):
    return pl.pallas_call(
        kernel,
        out_shape=outs,
        in_specs=in_specs,
        out_specs=[VMEM] * len(outs),
        cost_estimate=pl.CostEstimate(flops=flops, bytes_accessed=nbytes, transcendentals=0),
        compiler_params=pltpu.CompilerParams(vmem_limit_bytes=limit << 20),
    )


def add_pieces(a, b):
    out = jax.ShapeDtypeStruct(a.shape, a.dtype)
    return call(add_kernel, [VMEM] * 2, [out], a.size, 6 * a.size, 6)(a, b)[0]


def finish(own, keep_a, keep_b, recv_a, recv_b, x, rows):
    step = 128
    return pl.pallas_call(
        final_kernel,
        grid=(rows // step,),
        out_shape=jax.ShapeDtypeStruct((1, rows, C), jnp.bfloat16),
        in_specs=[SMEM] + [VMEM] * 4 + [pl.BlockSpec((1, step, C), lambda i: (0, i, 0))],
        out_specs=pl.BlockSpec((1, step, C), lambda i: (0, i, 0)),
        scratch_shapes=[
            pltpu.VMEM((C, C), jnp.bfloat16),
            pltpu.VMEM((C, C), jnp.bfloat16),
            pltpu.VMEM((8, H), jnp.float32),
        ],
        cost_estimate=pl.CostEstimate(flops=4 * rows * C * C, bytes_accessed=4 * rows * C, transcendentals=0),
        compiler_params=pltpu.CompilerParams(vmem_limit_bytes=24 << 20),
    )(own, keep_a, keep_b, recv_a, recv_b, x)


PAIR = [(0, 1), (1, 0), (2, 3), (3, 2)]
CROSS = [(1, 2), (2, 1), (0, 3), (3, 0)]
DP = ("z", "y_hi", "x", "core")
Z, Y_HI, X, CORES = 12, 2, 4, 2


def over(line, axes):
    count = lax.axis_size(axes)
    parts = lax.all_to_all(jnp.broadcast_to(line, (count, H)), axes, 0, 0, tiled=True)
    return jnp.sum(parts, axis=0, keepdims=True)


def step(gradient):
    rows = gradient.shape[1]
    place = lax.axis_index("slab")
    own = jnp.where((place == 1) | (place == 2), 1, 0).astype(jnp.int32).reshape(1)
    work = rows * B * B * 2
    send_a, tile = call(first_kernel, [SMEM, VMEM], [PART_A, TILE], 3 * work, 2 * rows * C, 16)(own, gradient)
    got_a = lax.ppermute(send_a, "slab", PAIR)
    (send_b,) = call(second_kernel, [SMEM, VMEM], [PART_B], 2 * work, 2 * rows * C, 16)(own, gradient)
    got_b = lax.ppermute(send_b, "slab", PAIR)
    keep_a, keep_b = call(third_kernel, [SMEM, VMEM], [PART_A, PART_B], 5 * work, 2 * rows * C, 16)(own, gradient)
    half_a = add_pieces(keep_a, got_a)
    crossed_a = lax.ppermute(half_a, "slab", CROSS)
    total = over(tile[0:1], ("y_hi", "slab"))
    total = over(total, ("z",))
    half_b = add_pieces(keep_b, got_b)
    crossed_b = lax.ppermute(half_b, "slab", CROSS)
    whole_a = add_pieces(half_a, crossed_a)
    other_a = lax.ppermute(whole_a, "slab", PAIR)
    whole_b = add_pieces(half_b, crossed_b)
    other_b = lax.ppermute(whole_b, "slab", PAIR)
    total = over(total, ("x", "core"))
    update = finish(own, whole_a, whole_b, other_a, other_b, gradient, rows)
    entries = gradient.size * lax.axis_size(DP) * lax.axis_size("slab")
    return update, jnp.sqrt(total[0, 0] / entries)


def solution(mesh):
    named = Mesh(mesh.devices.reshape(Z, Y_HI, X, CORES, mesh.shape["slab"]), DP + ("slab",))
    placed = P(DP, "slab", None)
    return jax.shard_map(step, mesh=named, in_specs=(placed,), out_specs=(placed, P()), check_vma=False)
```

```python
import math

import jax
import jax.numpy as jnp
from jax import lax
from jax.experimental import pallas as pl
from jax.experimental.pallas import tpu as pltpu
from jax.sharding import Mesh
from jax.sharding import PartitionSpec as P

R = 3584
C = 1024
B = 256
H = 128
REST = B + 16
LARGE = 2 * B + REST

FULL = ((1, 0), (2, 1), (3, 2), (3, 0))
HALF = ((2, 0, 0), (2, 0, 1), (3, 1, 0), (3, 1, 1))


def pick(p, values):
    out = jnp.int32(values[0])
    for k in range(1, len(values)):
        out = jnp.where(p == k, jnp.int32(values[k]), out)
    return out


def lower(shape=(H, H)):
    rows = lax.broadcasted_iota(jnp.int32, shape, 0)
    cols = lax.broadcasted_iota(jnp.int32, shape, 1)
    return rows, cols


def columns(x_ref, start, width):
    return x_ref[0, :, pl.ds(pl.multiple_of(start, H), width)]


def outer(a, b):
    return lax.dot_general(a, b, (((0,), (0,)), ((), ())), preferred_element_type=jnp.float32)


def whole_block(x_ref, p, out_ref, at):
    i, j = (pick(p, [f[k] for f in FULL]) for k in (0, 1))
    out_ref[at : at + B, :] = outer(columns(x_ref, i * B, B), columns(x_ref, j * B, B)).astype(jnp.bfloat16)


def rest(x_ref, p, out_ref, at):
    i, j, part = (pick(p, [h[k] for h in HALF]) for k in (0, 1, 2))
    out_ref[at : at + H, :] = outer(
        columns(x_ref, i * B + part * H, H), columns(x_ref, j * B, B)
    ).astype(jnp.bfloat16)
    own = columns(x_ref, p * B, B)
    diag = outer(own, own)
    rows, cols = lower()
    first, last = diag[:H, :H], diag[H:, H:]
    out_ref[at + H : at + B, :H] = diag[H:, :H].astype(jnp.bfloat16)
    out_ref[at + H : at + B, H:] = jnp.where(rows > cols, first, last).astype(jnp.bfloat16)
    line = jnp.sum(jnp.where(rows == cols, first, 0.0), axis=0, keepdims=True)
    line = jnp.broadcast_to(jnp.concatenate([line, line], axis=1), (16, B))
    out_ref[at + B : at + REST, :] = line.astype(jnp.bfloat16)


def large_part(x_ref, half, out_ref):
    whole_block(x_ref, 2 * half, out_ref, 0)
    rest(x_ref, 2 * half, out_ref, B)
    whole_block(x_ref, 2 * half + 1, out_ref, B + REST)


def first_kernel(own_ref, x_ref, out_ref, sum_ref):
    wide = x_ref[0].astype(jnp.float32)
    squares = jnp.sum(wide * wide, axis=0, keepdims=True)
    total = jnp.sum(squares, axis=1, keepdims=True)
    sum_ref[...] = jnp.broadcast_to(total, (8, H))
    large_part(x_ref, 1 - own_ref[0], out_ref)


def second_kernel(own_ref, x_ref, out_ref):
    rest(x_ref, 2 * (1 - own_ref[0]) + 1, out_ref, 0)


def third_kernel(own_ref, x_ref, keep_a_ref, keep_b_ref):
    large_part(x_ref, own_ref[0], keep_a_ref)
    rest(x_ref, 2 * own_ref[0] + 1, keep_b_ref, 0)


def add_kernel(a_ref, b_ref, out_ref):
    out_ref[...] = (a_ref[...].astype(jnp.float32) + b_ref[...].astype(jnp.float32)).astype(jnp.bfloat16)


def final_kernel(own_ref, keep_a_ref, keep_b_ref, recv_a_ref, recv_b_ref, x_ref, out_ref, gram, poly, done, sems):
    mine = own_ref[0] == 0
    rows, cols = lower()
    squares = jnp.zeros((H, B), jnp.float32)
    for p in range(4):
        low = p < 2

        def get(small, start, size):
            keep_ref, recv_ref = (keep_b_ref, recv_b_ref) if small else (keep_a_ref, recv_a_ref)
            k, r = keep_ref[start : start + size, :], recv_ref[start : start + size, :]
            return jnp.where(mine, k, r) if low else jnp.where(mine, r, k)

        small = p % 2 == 1
        top, base = (B + REST, 0) if small else (0, B)

        def put(i, j, block):
            gram[i : i + block.shape[0], j : j + block.shape[1]] = block
            gram[j : j + block.shape[1], i : i + block.shape[0]] = block.T

        block = get(False, top, B)
        fi, fj = FULL[p]
        put(fi * B, fj * B, block)
        wide = block.astype(jnp.float32)
        squares += 2.0 * (wide[:H] * wide[:H] + wide[H:] * wide[H:])
        block = get(small, base, H)
        hi, hj, part = HALF[p]
        put(hi * B + part * H, hj * B, block)
        wide = block.astype(jnp.float32)
        squares += 2.0 * wide * wide
        block = get(small, base + H, H)
        put(p * B + H, p * B, block[:, :H])
        fold = block[:, H:].astype(jnp.float32)
        flip = fold.T
        line = get(small, base + B, 16)[0:1, :H].astype(jnp.float32)
        upper = jnp.where(rows < cols, flip, jnp.where(rows == cols, jnp.broadcast_to(line, (H, H)), fold))
        second = jnp.where(rows > cols, flip, fold)
        gram[p * B : p * B + H, p * B : p * B + H] = upper.astype(jnp.bfloat16)
        gram[p * B + H : (p + 1) * B, p * B + H : (p + 1) * B] = second.astype(jnp.bfloat16)
        wide = block[:, :H].astype(jnp.float32)
        squares += jnp.concatenate([2.0 * wide * wide, upper * upper + second * second], axis=1)
    norm = jnp.sqrt(jnp.sum(jnp.sum(squares, axis=0, keepdims=True), axis=1, keepdims=True))
    factor = 1.0 / (norm + 1e-07)
    for j in range(4):
        cols = slice(j * B, (j + 1) * B)
        product = jnp.dot(gram[j * B :, :], gram[:, cols], preferred_element_type=jnp.float32)
        block = gram[j * B :, cols].astype(jnp.float32)
        block = (-4.775 * factor * block + 2.0315 * factor * factor * product).astype(jnp.bfloat16)
        poly[j * B :, cols] = block
        for i in range(j + 1, 4):
            poly[cols, i * B : (i + 1) * B] = block[(i - j) * B : (i - j + 1) * B, :].T

    scale = math.sqrt(R) * jnp.sqrt(factor)
    copies = []
    for j in range(4):
        cols = slice(j * B, (j + 1) * B)
        applied = jnp.dot(x_ref[0], poly[:, cols], preferred_element_type=jnp.float32)
        done[0, :, cols] = (scale * (3.4445 * x_ref[0, :, cols].astype(jnp.float32) + applied)).astype(jnp.bfloat16)
        copies.append(pltpu.make_async_copy(done.at[:, :, cols], out_ref.at[:, :, cols], sems.at[j]))
        copies[-1].start()
    for copy in copies:
        copy.wait()


PART_A = jax.ShapeDtypeStruct((LARGE, B), jnp.bfloat16)
PART_B = jax.ShapeDtypeStruct((REST, B), jnp.bfloat16)
TILE = jax.ShapeDtypeStruct((8, H), jnp.float32)
SMEM = pl.BlockSpec(memory_space=pltpu.SMEM)
VMEM = pl.BlockSpec(memory_space=pltpu.VMEM)


def call(kernel, in_specs, outs, flops, nbytes, limit):
    return pl.pallas_call(
        kernel,
        out_shape=outs,
        in_specs=in_specs,
        out_specs=[VMEM] * len(outs),
        cost_estimate=pl.CostEstimate(flops=flops, bytes_accessed=nbytes, transcendentals=0),
        compiler_params=pltpu.CompilerParams(vmem_limit_bytes=limit << 20),
    )


def add_pieces(a, b):
    out = jax.ShapeDtypeStruct(a.shape, a.dtype)
    return call(add_kernel, [VMEM] * 2, [out], a.size, 6 * a.size, 6)(a, b)[0]


def finish(own, keep_a, keep_b, recv_a, recv_b, x, rows):
    return pl.pallas_call(
        final_kernel,
        out_shape=jax.ShapeDtypeStruct((1, rows, C), jnp.bfloat16),
        in_specs=[SMEM] + [VMEM] * 5,
        out_specs=pl.BlockSpec(memory_space=pl.ANY),
        scratch_shapes=[
            pltpu.VMEM((C, C), jnp.bfloat16),
            pltpu.VMEM((C, C), jnp.bfloat16),
            pltpu.VMEM((1, rows, C), jnp.bfloat16),
            pltpu.SemaphoreType.DMA((4,)),
        ],
        cost_estimate=pl.CostEstimate(flops=4 * rows * C * C, bytes_accessed=4 * rows * C, transcendentals=0),
        compiler_params=pltpu.CompilerParams(vmem_limit_bytes=32 << 20),
    )(own, keep_a, keep_b, recv_a, recv_b, x)


PAIR = [(0, 1), (1, 0), (2, 3), (3, 2)]
CROSS = [(1, 2), (2, 1), (0, 3), (3, 0)]
DP = ("z", "y_hi", "x", "core")
Z, Y_HI, X, CORES = 12, 2, 4, 2


def over(line, axes):
    count = lax.axis_size(axes)
    lines = line if line.shape[0] == count else jnp.broadcast_to(line, (count, H))
    parts = lax.all_to_all(lines, axes, 0, 0, tiled=True)
    return jnp.sum(parts, axis=0, keepdims=True)


def step(gradient):
    rows = gradient.shape[1]
    place = lax.axis_index("slab")
    own = jnp.where((place == 1) | (place == 2), 1, 0).astype(jnp.int32).reshape(1)
    work = rows * B * B * 2
    send_a, tile = call(first_kernel, [SMEM, VMEM], [PART_A, TILE], 3 * work, 2 * rows * C, 16)(own, gradient)
    got_a = lax.ppermute(send_a, "slab", PAIR)
    (send_b,) = call(second_kernel, [SMEM, VMEM], [PART_B], 2 * work, 2 * rows * C, 16)(own, gradient)
    got_b = lax.ppermute(send_b, "slab", PAIR)
    keep_a, keep_b = call(third_kernel, [SMEM, VMEM], [PART_A, PART_B], 5 * work, 2 * rows * C, 16)(own, gradient)
    half_a = add_pieces(keep_a, got_a)
    crossed_a = lax.ppermute(half_a, "slab", CROSS)
    total = over(tile, ("y_hi", "slab"))
    total = over(total, ("z",))
    half_b = add_pieces(keep_b, got_b)
    crossed_b = lax.ppermute(half_b, "slab", CROSS)
    whole_a = add_pieces(half_a, crossed_a)
    other_a = lax.ppermute(whole_a, "slab", PAIR)
    whole_b = add_pieces(half_b, crossed_b)
    other_b = lax.ppermute(whole_b, "slab", PAIR)
    total = over(total, ("x", "core"))
    update = finish(own, whole_a, whole_b, other_a, other_b, gradient, rows)
    entries = gradient.size * lax.axis_size(DP) * lax.axis_size("slab")
    return update, jnp.sqrt(total[0, 0] / entries)


def solution(mesh):
    named = Mesh(mesh.devices.reshape(Z, Y_HI, X, CORES, mesh.shape["slab"]), DP + ("slab",))
    placed = P(DP, "slab", None)
    return jax.shard_map(step, mesh=named, in_specs=(placed,), out_specs=(placed, P()), check_vma=False)
```

```python
import functools
import math

import jax
import jax.numpy as jnp
from jax import lax
from jax.experimental import pallas as pl
from jax.experimental.pallas import tpu as pltpu
from jax.sharding import Mesh
from jax.sharding import PartitionSpec as P

R = 3584
C = 1024
B = 256
H = 128
REST = B + 16
LARGE = 2 * B + REST

FULL = ((1, 0), (2, 1), (3, 2), (3, 0))
HALF = ((2, 0, 0), (2, 0, 1), (3, 1, 0), (3, 1, 1))


def pick(p, values):
    out = jnp.int32(values[0])
    for k in range(1, len(values)):
        out = jnp.where(p == k, jnp.int32(values[k]), out)
    return out


def lower(shape=(H, H)):
    rows = lax.broadcasted_iota(jnp.int32, shape, 0)
    cols = lax.broadcasted_iota(jnp.int32, shape, 1)
    return rows, cols


def columns(x_ref, start, width):
    return x_ref[0, :, pl.ds(pl.multiple_of(start, H), width)]


def outer(a, b):
    return lax.dot_general(a, b, (((0,), (0,)), ((), ())), preferred_element_type=jnp.float32)


def whole_block(x_ref, p, out_ref, at):
    i, j = (pick(p, [f[k] for f in FULL]) for k in (0, 1))
    out_ref[at : at + B, :] = outer(columns(x_ref, i * B, B), columns(x_ref, j * B, B)).astype(jnp.bfloat16)


def rest(x_ref, p, out_ref, at):
    i, j, part = (pick(p, [h[k] for h in HALF]) for k in (0, 1, 2))
    out_ref[at : at + H, :] = outer(
        columns(x_ref, i * B + part * H, H), columns(x_ref, j * B, B)
    ).astype(jnp.bfloat16)
    own = columns(x_ref, p * B, B)
    diag = outer(own, own)
    rows, cols = lower()
    first, last = diag[:H, :H], diag[H:, H:]
    out_ref[at + H : at + B, :H] = diag[H:, :H].astype(jnp.bfloat16)
    out_ref[at + H : at + B, H:] = jnp.where(rows > cols, first, last).astype(jnp.bfloat16)
    line = jnp.sum(jnp.where(rows == cols, first, 0.0), axis=0, keepdims=True)
    line = jnp.broadcast_to(jnp.concatenate([line, line], axis=1), (16, B))
    out_ref[at + B : at + REST, :] = line.astype(jnp.bfloat16)


def large_part(x_ref, half, out_ref):
    whole_block(x_ref, 2 * half, out_ref, 0)
    rest(x_ref, 2 * half, out_ref, B)
    whole_block(x_ref, 2 * half + 1, out_ref, B + REST)


def first_kernel(own_ref, x_ref, out_ref):
    large_part(x_ref, 1 - own_ref[0], out_ref)


def second_kernel(own_ref, x_ref, out_ref, sum_ref):
    wide = x_ref[0].astype(jnp.float32)
    squares = jnp.sum(wide * wide, axis=0, keepdims=True)
    total = jnp.sum(squares, axis=1, keepdims=True)
    sum_ref[...] = jnp.broadcast_to(total, (8, H))
    rest(x_ref, 2 * (1 - own_ref[0]) + 1, out_ref, 0)


def third_kernel(own_ref, x_ref, keep_a_ref, keep_b_ref):
    large_part(x_ref, own_ref[0], keep_a_ref)
    rest(x_ref, 2 * own_ref[0] + 1, keep_b_ref, 0)


def add_kernel(a_ref, b_ref, out_ref):
    out_ref[...] = (a_ref[...].astype(jnp.float32) + b_ref[...].astype(jnp.float32)).astype(jnp.bfloat16)


def final_kernel(own_ref, keep_a_ref, keep_b_ref, recv_a_ref, recv_b_ref, x_ref, out_ref, gram, poly, done, sems):
    mine = own_ref[0] == 0
    rows, cols = lower()
    squares = jnp.zeros((H, B), jnp.float32)
    for p in range(4):
        low = p < 2

        def get(small, start, size):
            keep_ref, recv_ref = (keep_b_ref, recv_b_ref) if small else (keep_a_ref, recv_a_ref)
            k, r = keep_ref[start : start + size, :], recv_ref[start : start + size, :]
            return jnp.where(mine, k, r) if low else jnp.where(mine, r, k)

        small = p % 2 == 1
        top, base = (B + REST, 0) if small else (0, B)

        def put(i, j, block):
            gram[i : i + block.shape[0], j : j + block.shape[1]] = block
            gram[j : j + block.shape[1], i : i + block.shape[0]] = block.T

        block = get(False, top, B)
        fi, fj = FULL[p]
        put(fi * B, fj * B, block)
        wide = block.astype(jnp.float32)
        squares += 2.0 * (wide[:H] * wide[:H] + wide[H:] * wide[H:])
        block = get(small, base, H)
        hi, hj, part = HALF[p]
        put(hi * B + part * H, hj * B, block)
        wide = block.astype(jnp.float32)
        squares += 2.0 * wide * wide
        block = get(small, base + H, H)
        put(p * B + H, p * B, block[:, :H])
        fold = block[:, H:].astype(jnp.float32)
        flip = fold.T
        line = get(small, base + B, 16)[0:1, :H].astype(jnp.float32)
        upper = jnp.where(rows < cols, flip, jnp.where(rows == cols, jnp.broadcast_to(line, (H, H)), fold))
        second = jnp.where(rows > cols, flip, fold)
        gram[p * B : p * B + H, p * B : p * B + H] = upper.astype(jnp.bfloat16)
        gram[p * B + H : (p + 1) * B, p * B + H : (p + 1) * B] = second.astype(jnp.bfloat16)
        wide = block[:, :H].astype(jnp.float32)
        squares += jnp.concatenate([2.0 * wide * wide, upper * upper + second * second], axis=1)
    norm = jnp.sqrt(jnp.sum(jnp.sum(squares, axis=0, keepdims=True), axis=1, keepdims=True))
    factor = 1.0 / (norm + 1e-07)
    for j in range(4):
        cols = slice(j * B, (j + 1) * B)
        product = jnp.dot(gram[j * B :, :], gram[:, cols], preferred_element_type=jnp.float32)
        block = gram[j * B :, cols].astype(jnp.float32)
        block = (-4.775 * factor * block + 2.0315 * factor * factor * product).astype(jnp.bfloat16)
        poly[j * B :, cols] = block
        for i in range(j + 1, 4):
            poly[cols, i * B : (i + 1) * B] = block[(i - j) * B : (i - j + 1) * B, :].T

    scale = math.sqrt(R) * jnp.sqrt(factor)
    copies = []
    for j in range(4):
        cols = slice(j * B, (j + 1) * B)
        applied = jnp.dot(x_ref[0], poly[:, cols], preferred_element_type=jnp.float32)
        done[0, :, cols] = (scale * (3.4445 * x_ref[0, :, cols].astype(jnp.float32) + applied)).astype(jnp.bfloat16)
        copies.append(pltpu.make_async_copy(done.at[:, :, cols], out_ref.at[:, :, cols], sems.at[j]))
        copies[-1].start()
    for copy in copies:
        copy.wait()


PART_A = jax.ShapeDtypeStruct((LARGE, B), jnp.bfloat16)
PART_B = jax.ShapeDtypeStruct((REST, B), jnp.bfloat16)
TILE = jax.ShapeDtypeStruct((8, H), jnp.float32)
SMEM = pl.BlockSpec(memory_space=pltpu.SMEM)
VMEM = pl.BlockSpec(memory_space=pltpu.VMEM)


def call(kernel, in_specs, outs, flops, nbytes, limit):
    return pl.pallas_call(
        kernel,
        out_shape=outs,
        in_specs=in_specs,
        out_specs=[VMEM] * len(outs),
        cost_estimate=pl.CostEstimate(flops=flops, bytes_accessed=nbytes, transcendentals=0),
        compiler_params=pltpu.CompilerParams(vmem_limit_bytes=limit << 20),
    )


def add_pieces(a, b):
    out = jax.ShapeDtypeStruct(a.shape, a.dtype)
    return call(add_kernel, [VMEM] * 2, [out], a.size, 6 * a.size, 6)(a, b)[0]


def finish(own, keep_a, keep_b, recv_a, recv_b, x, rows):
    return pl.pallas_call(
        final_kernel,
        out_shape=jax.ShapeDtypeStruct((1, rows, C), jnp.bfloat16),
        in_specs=[SMEM] + [VMEM] * 5,
        out_specs=pl.BlockSpec(memory_space=pl.ANY),
        scratch_shapes=[
            pltpu.VMEM((C, C), jnp.bfloat16),
            pltpu.VMEM((C, C), jnp.bfloat16),
            pltpu.VMEM((1, rows, C), jnp.bfloat16),
            pltpu.SemaphoreType.DMA((4,)),
        ],
        cost_estimate=pl.CostEstimate(flops=4 * rows * C * C, bytes_accessed=4 * rows * C, transcendentals=0),
        compiler_params=pltpu.CompilerParams(vmem_limit_bytes=32 << 20),
    )(own, keep_a, keep_b, recv_a, recv_b, x)


PAIR = [(0, 1), (1, 0), (2, 3), (3, 2)]
CROSS = [(1, 2), (2, 1), (0, 3), (3, 0)]
DP = ("z", "y_hi", "x", "core")
Z, Y_HI, X, CORES = 12, 2, 4, 2


def root_kernel(entries, parts_ref, out_ref):
    total = jnp.sum(parts_ref[...], axis=0, keepdims=True)
    out_ref[...] = jnp.sqrt(total[:, 0:1] / entries)


def parts_over(line, axes):
    count = lax.axis_size(axes)
    lines = line if line.shape[0] == count else jnp.broadcast_to(line, (count, H))
    return lax.all_to_all(lines, axes, 0, 0, tiled=True)


def over(line, axes):
    return jnp.sum(parts_over(line, axes), axis=0, keepdims=True)


def step(gradient):
    rows = gradient.shape[1]
    place = lax.axis_index("slab")
    own = jnp.where((place == 1) | (place == 2), 1, 0).astype(jnp.int32).reshape(1)
    work = rows * B * B * 2
    (send_a,) = call(first_kernel, [SMEM, VMEM], [PART_A], 3 * work, 2 * rows * C, 16)(own, gradient)
    got_a = lax.ppermute(send_a, "slab", PAIR)
    send_b, tile = call(second_kernel, [SMEM, VMEM], [PART_B, TILE], 2 * work, 2 * rows * C, 16)(own, gradient)
    got_b = lax.ppermute(send_b, "slab", PAIR)
    keep_a, keep_b = call(third_kernel, [SMEM, VMEM], [PART_A, PART_B], 5 * work, 2 * rows * C, 16)(own, gradient)
    half_a = add_pieces(keep_a, got_a)
    crossed_a = lax.ppermute(half_a, "slab", CROSS)
    total = over(tile, ("y_hi", "slab"))
    total = over(total, ("z",))
    half_b = add_pieces(keep_b, got_b)
    crossed_b = lax.ppermute(half_b, "slab", CROSS)
    whole_a = add_pieces(half_a, crossed_a)
    other_a = lax.ppermute(whole_a, "slab", PAIR)
    whole_b = add_pieces(half_b, crossed_b)
    other_b = lax.ppermute(whole_b, "slab", PAIR)
    parts = parts_over(total, ("x", "core"))
    update = finish(own, whole_a, whole_b, other_a, other_b, gradient, rows)
    entries = gradient.size * lax.axis_size(DP) * lax.axis_size("slab")
    root = functools.partial(root_kernel, float(entries))
    (rms,) = call(root, [VMEM], [jax.ShapeDtypeStruct((1, 1), jnp.float32)], 8 * H, 32 * H, 1)(parts)
    return update, rms.reshape(())


def solution(mesh):
    named = Mesh(mesh.devices.reshape(Z, Y_HI, X, CORES, mesh.shape["slab"]), DP + ("slab",))
    placed = P(DP, "slab", None)
    return jax.shard_map(step, mesh=named, in_specs=(placed,), out_specs=(placed, P()), check_vma=False)
```
